32 devices in a mesh: dp: 8 (over z, x), tensor: 4 (over y, core).
Axes of the slice: x: 2, y: 2, z: 4, core: 2. Of those that a mesh axis runs over, the one named last changes fastest.
Arguments:
- tokens: bfloat16 [4096, 1024], P('dp'), may hold values from -6 to 6
- norm1_gain: float32 [1024], replicated, may hold values from 0.25 to 1.75
- in_weight: bfloat16 [1024, 3, 1024], P(None, None, 'tensor'), may hold values from -0.1875 to 0.1875
- conv_weight: float32 [3, 1024], P(None, 'tensor'), may hold values from -3 to 3
- out_weight: bfloat16 [1024, 1024], P('tensor'), may hold values from -0.1875 to 0.1875
- norm2_gain: float32 [1024], replicated, may hold values from 0.25 to 1.75
- gate_weight: bfloat16 [1024, 4608], P(None, 'tensor'), may hold values from -0.1875 to 0.1875
- up_weight: bfloat16 [1024, 4608], P(None, 'tensor'), may hold values from -0.1875 to 0.1875
- down_weight: bfloat16 [4608, 1024], P('tensor'), may hold values from -0.09375 to 0.09375
- cotangent: bfloat16 [4096, 1024], P('dp'), may hold values from -6 to 6
Outputs:
- block_output: bfloat16 [4096, 1024], P('dp')
- input_grad: float32 [4096, 1024], P('dp')
- norm1_grad: float32 [1024], replicated
- in_grad: float32 [1024, 3, 1024], P('dp', None, 'tensor')
- conv_grad: float32 [3, 1024], P(None, 'tensor')
- out_grad: float32 [1024, 1024], P('tensor', 'dp')
- norm2_grad: float32 [1024], replicated
- gate_grad: float32 [1024, 4608], P('dp', 'tensor')
- up_grad: float32 [1024, 4608], P('dp', 'tensor')
- down_grad: float32 [4608, 1024], P('tensor', 'dp')
The draws below stay inside these ranges and needn't reach their ends.
All inputs are finite; a program needn't handle non-finite values.
Results may differ from the reference program's by a relative error of at most 0.02.
Values may be sent and summed in bfloat16 or wider, within the bound.
No kernel may reach another device: no remote copies, remote signals or barrier semaphores. Data moves between devices by JAX's collectives and lax.ppermute only.
A program may use at most 128 MiB of HBM per device.

```python
import jax
import jax.numpy as jnp
from jax import lax

D = 1024
FF = 4608
KW = 3
SEQ = 512
TOKENS = 4096
N_TENSOR = 4


def strengthened(drawn, stream_key, source, target, blocks, factor):
    def block_of(axis_at):
        return (jnp.arange(drawn.shape[axis_at]) // (drawn.shape[axis_at] // blocks)).reshape((-1,) + (1,) * (drawn.ndim - 1 - axis_at))

    near = jax.random.permutation(stream_key, blocks)[block_of(target)]
    far = (block_of(target) + blocks // 2) % blocks
    return jnp.where((block_of(source) == near) | (block_of(source) == far), factor * drawn, drawn)


def block_scale(key, extent, pieces, low, largest):
    def one(axis_at, shards_of):
        heights = jax.random.uniform(jax.random.fold_in(jax.random.fold_in(key, 6), axis_at), (shards_of,), jnp.float32, low / len(pieces), largest / len(pieces))
        return jnp.repeat(jnp.exp(heights), extent[axis_at] // shards_of).reshape((-1,) + (1,) * (len(extent) - axis_at - 1))

    level = one(*pieces[0])
    for cut in pieces[1:]:
        level = level * one(*cut)
    return level


def gaussian(own_key, dims, scale, reach, shards=(), held_as=jnp.bfloat16):
    entries = scale * jax.random.normal(own_key, dims, jnp.float32)
    if shards:
        entries = entries * block_scale(own_key, dims, shards, -0.22, 0.18)
    return jnp.clip(entries, -reach, reach).astype(held_as)


def gaussian_with(rng, dims, deviation, reach, cuts, heavy, kind=jnp.bfloat16):
    result = deviation * jax.random.normal(rng, dims, jnp.float32)
    if cuts:
        result = result * block_scale(rng, dims, cuts, -0.22, 0.18)
    return jnp.clip(strengthened(result, jax.random.fold_in(rng, 3), *heavy), -reach, reach).astype(kind)


def setup_inputs(seed: int = 0) -> dict:
    key_list = jax.random.split(jax.random.key(seed), 11)
    tokens = gaussian(key_list[0], (TOKENS, D), 1.0, 6.0, ((0, 8),))
    norm1_gain = jnp.clip(1.0 + 0.15 * jax.random.normal(key_list[1], (D,), jnp.float32), 0.25, 1.75)
    in_weight = gaussian(key_list[2], (D, 3, D), D ** -0.5, 0.1875, ((2, 4),))
    conv_weight = gaussian(key_list[3], (KW, D), 0.6, 3.0, ((1, 4),), jnp.float32)
    out_weight = gaussian(key_list[4], (D, D), D ** -0.5, 0.1875, ((0, 4),))
    norm2_gain = jnp.clip(1.0 + 0.15 * jax.random.normal(key_list[5], (D,), jnp.float32), 0.25, 1.75)
    gate_weight = gaussian(key_list[6], (D, FF), D ** -0.5, 0.1875, ((1, 4),))
    up_weight = gaussian(key_list[7], (D, FF), D ** -0.5, 0.1875, ((1, 4),))
    down_weight = gaussian(key_list[8], (FF, D), FF ** -0.5, 0.09375, ((0, 4),))
    cotangent = gaussian_with(key_list[9], (TOKENS, D), 1.0, 6.0, ((0, 8),), (0, 1, 8, 2.0))
    return {"tokens": tokens, "norm1_gain": norm1_gain, "in_weight": in_weight, "conv_weight": conv_weight, "out_weight": out_weight, "norm2_gain": norm2_gain, "gate_weight": gate_weight, "up_weight": up_weight, "down_weight": down_weight, "cotangent": cotangent}


epsilon = 1e-05

def rms_scale(values):
    return lax.rsqrt(lax.optimization_barrier(jnp.mean(values * values, axis=-1, keepdims=True)) + epsilon)

def round_partials(parts):
    rounded = lax.optimization_barrier(parts.astype(jnp.bfloat16))
    return lax.optimization_barrier(jnp.sum(rounded.astype(jnp.float32), axis=0))

def split_sum(left, right):
    row_count, inner = left.shape
    group = inner // N_TENSOR
    parts = jnp.einsum('snk,nkm->nsm', left.reshape(row_count, N_TENSOR, group).astype(jnp.float32), right.reshape(N_TENSOR, group, right.shape[1]).astype(jnp.float32))
    return round_partials(parts)

def split_back(left, right):
    row_count, stacked, inner = left.shape
    group = inner // N_TENSOR
    parts = jnp.einsum('sjnk,djnk->nsd', left.reshape(row_count, stacked, N_TENSOR, group).astype(jnp.float32), right.reshape(right.shape[0], stacked, N_TENSOR, group).astype(jnp.float32))
    return round_partials(parts)

def shift_down(values, offset):
    return jnp.pad(values[:values.shape[0] - offset], ((offset, 0), (0, 0)))

def shift_up(values, offset):
    return jnp.pad(values[offset:], ((0, offset), (0, 0)))

def reference(tokens, norm1_gain, in_weight, conv_weight, out_weight, norm2_gain, gate_weight, up_weight, down_weight, cotangent):

    def sequence_pass(carry, batch):
        inputs, grad_rows = batch
        inputs_wide = inputs.astype(jnp.float32)
        scale_one = rms_scale(inputs_wide)
        normed_one = (inputs_wide * scale_one * norm1_gain).astype(jnp.bfloat16)
        projected = jnp.dot(normed_one, in_weight.reshape(D, 3 * D), preferred_element_type=jnp.float32).reshape(SEQ, 3, D)
        gate_b = projected[:, 0]
        gate_c = projected[:, 1]
        values = projected[:, 2]
        mixed = gate_b * values
        conv_out = jnp.zeros((SEQ, D), jnp.float32)
        for offset in range(KW):
            conv_out = conv_out + conv_weight[offset] * shift_down(mixed, KW - 1 - offset)
        mixer = (gate_c * conv_out).astype(jnp.bfloat16)
        resid = inputs_wide + split_sum(mixer, out_weight)
        scale_two = rms_scale(resid)
        normed_two = (resid * scale_two * norm2_gain).astype(jnp.bfloat16)
        gate_pre = jnp.dot(normed_two, gate_weight, preferred_element_type=jnp.float32)
        up_pre = jnp.dot(normed_two, up_weight, preferred_element_type=jnp.float32)
        sigma = jax.nn.sigmoid(gate_pre)
        activated = (gate_pre * sigma * up_pre).astype(jnp.bfloat16)
        output = (resid + split_sum(activated, down_weight)).astype(jnp.bfloat16)
        grad_wide = grad_rows.astype(jnp.float32)
        down_part = jnp.dot(activated.T, grad_rows, preferred_element_type=jnp.float32)
        d_act = jnp.dot(grad_rows, down_weight.T, preferred_element_type=jnp.float32)
        d_gate = (d_act * up_pre * sigma * (1.0 + gate_pre * (1.0 - sigma))).astype(jnp.bfloat16)
        d_up = (d_act * gate_pre * sigma).astype(jnp.bfloat16)
        gate_part = jnp.dot(normed_two.T, d_gate, preferred_element_type=jnp.float32)
        up_part = jnp.dot(normed_two.T, d_up, preferred_element_type=jnp.float32)
        d_normed_two = split_back(jnp.stack([d_gate, d_up], axis=1), jnp.stack([gate_weight, up_weight], axis=1))
        norm2_part = lax.optimization_barrier(jnp.sum(d_normed_two * resid * scale_two, axis=0))
        scaled_two = d_normed_two * norm2_gain
        d_resid = grad_wide + scale_two * scaled_two - resid * scale_two ** 3 * lax.optimization_barrier(jnp.mean(scaled_two * resid, axis=-1, keepdims=True))
        d_resid_b = d_resid.astype(jnp.bfloat16)
        out_part = jnp.dot(mixer.T, d_resid_b, preferred_element_type=jnp.float32)
        d_mixer = jnp.dot(d_resid_b, out_weight.T, preferred_element_type=jnp.float32)
        d_gate_c = d_mixer * conv_out
        d_conv = d_mixer * gate_c
        conv_rows = []
        d_mixed = jnp.zeros((SEQ, D), jnp.float32)
        for offset in range(KW):
            conv_rows.append(lax.optimization_barrier(jnp.sum(d_conv * shift_down(mixed, KW - 1 - offset), axis=0)))
            d_mixed = d_mixed + conv_weight[offset] * shift_up(d_conv, KW - 1 - offset)
        conv_part = jnp.stack(conv_rows, axis=0)
        d_proj = jnp.stack([d_mixed * values, d_gate_c, d_mixed * gate_b], axis=1).astype(jnp.bfloat16)
        in_part = jnp.dot(normed_one.T, d_proj.reshape(SEQ, 3 * D), preferred_element_type=jnp.float32).reshape(D, 3, D)
        d_normed_one = split_back(d_proj, in_weight)
        norm1_part = lax.optimization_barrier(jnp.sum(d_normed_one * inputs_wide * scale_one, axis=0))
        scaled_one = d_normed_one * norm1_gain
        d_inputs = d_resid + scale_one * scaled_one - inputs_wide * scale_one ** 3 * lax.optimization_barrier(jnp.mean(scaled_one * inputs_wide, axis=-1, keepdims=True))
        parts = (norm1_part, in_part, conv_part, out_part, norm2_part, gate_part, up_part, down_part)
        new_carry = tuple((total + part for total, part in zip(carry, parts)))
        return (new_carry, (output, d_inputs))
    start = (jnp.zeros((D,), jnp.float32), jnp.zeros((D, 3, D), jnp.float32), jnp.zeros((KW, D), jnp.float32), jnp.zeros((D, D), jnp.float32), jnp.zeros((D,), jnp.float32), jnp.zeros((D, FF), jnp.float32), jnp.zeros((D, FF), jnp.float32), jnp.zeros((FF, D), jnp.float32))
    totals, (outputs, d_inputs) = lax.scan(sequence_pass, start, (tokens.reshape(TOKENS // SEQ, SEQ, D), cotangent.reshape(TOKENS // SEQ, SEQ, D)))
    return (outputs.reshape(TOKENS, D), d_inputs.reshape(TOKENS, D), totals[0], totals[1], totals[2], totals[3], totals[4], totals[5], totals[6], totals[7])
```

```python
import jax
import jax.numpy as jnp
from jax import lax
from jax.sharding import PartitionSpec as P

KW = 3
SEQ = 512
epsilon = 1e-05
wide = jnp.float32
narrow = jnp.bfloat16


def rms_scale(values):
    return lax.rsqrt(jnp.mean(values * values, axis=-1, keepdims=True) + epsilon)


def product(left, right):
    return jnp.dot(left, right, preferred_element_type=wide)


def product_back(left, right):
    return lax.dot_general(left, right, (((1,), (1,)), ((), ())), preferred_element_type=wide)


def inner_rows(left, right):
    return lax.dot_general(left, right, (((0,), (0,)), ((), ())), preferred_element_type=wide)


def shift_down(values, offset):
    return jnp.pad(values[:, : values.shape[1] - offset], ((0, 0), (offset, 0), (0, 0)))


def shift_up(values, offset):
    return jnp.pad(values[:, offset:], ((0, 0), (0, offset), (0, 0)))


def bits_of(size):
    count = size.bit_length() - 1
    assert size == 1 << count, size
    return list(range(count))


def flip(value, axis, size, bit):
    return lax.ppermute(value, axis, [(i, i ^ (1 << bit)) for i in range(size)])


def halving_order(bits):
    order = [0]
    for bit in reversed(bits):
        order = order + [place | (1 << bit) for place in order]
    return order


def relative_blocks(value, places, size, me):
    width = value.shape[1] // size
    return jnp.concatenate(
        [lax.dynamic_slice_in_dim(value, (place ^ me) * width, width, 1) for place in places], axis=1
    )


def make_body(n_dp, n_tensor):
    dp_bits = bits_of(n_dp)
    tensor_bits = bits_of(n_tensor)
    far_bits = tensor_bits[1:]

    def scatter_sum(by_dp, other, bits, columns):
        me = lax.axis_index("dp")
        order = halving_order(bits)
        half = n_dp // 2

        def part(places):
            mine = relative_blocks(by_dp, places, n_dp, me)
            return inner_rows(other, mine) if columns else inner_rows(mine, other)

        axis = 1 if columns else 0
        sent = part(order[half:]).astype(narrow)
        came = flip(sent, "dp", n_dp, bits[0])
        held = part(order[:half]) + came.astype(wide)
        for bit in bits[1:]:
            held = held.astype(narrow)
            middle = held.shape[axis] // 2
            kept, sent = jnp.split(held, [middle], axis=axis)
            came = flip(sent, "dp", n_dp, bit)
            held = kept.astype(wide) + came.astype(wide)
        return held

    def all_sum(value, axis, size, bits):
        for bit in bits:
            value = value + flip(value, axis, size, bit)
        return value

    def half_sum(left_mine, left_other, multiply):
        sent = multiply(left_other).astype(narrow)
        came = flip(sent, "tensor", n_tensor, 0)
        held = multiply(left_mine) + came.astype(wide)
        for bit in far_bits:
            sent = held.astype(narrow)
            held = sent.astype(wide) + flip(sent, "tensor", n_tensor, bit).astype(wide)
        return held

    def body(
        tokens,
        norm1_gain,
        in_weight,
        conv_weight,
        out_weight,
        norm2_gain,
        gate_weight,
        up_weight,
        down_weight,
        cotangent,
    ):
        rows_here, model_width = tokens.shape
        local_width = in_weight.shape[2]
        sequences = rows_here // SEQ
        half_rows = rows_here // 2
        core = lax.axis_index("tensor") % 2

        def mine(value):
            return lax.dynamic_slice_in_dim(value, core * half_rows, half_rows, 0)

        def others(value):
            return lax.dynamic_slice_in_dim(value, (1 - core) * half_rows, half_rows, 0)

        def whole(value):
            came = flip(value, "tensor", n_tensor, 0)
            first = jnp.where(core == 0, value, came)
            second = jnp.where(core == 0, came, value)
            return jnp.concatenate([first, second], axis=0)

        x_first = dp_bits
        z_first = dp_bits[1:] + dp_bits[:1]

        inputs_wide = tokens.astype(wide)
        scale_one = rms_scale(inputs_wide)
        normed_one = (inputs_wide * scale_one * norm1_gain).astype(narrow)
        flat_in = in_weight.reshape(model_width, 3 * local_width)
        projected = product(normed_one, flat_in).reshape(rows_here, 3, local_width)
        gate_b = projected[:, 0]
        gate_c = projected[:, 1]
        values = projected[:, 2]
        mixed = (gate_b * values).reshape(sequences, SEQ, local_width)
        conv_out = jnp.zeros_like(mixed)
        for offset in range(KW):
            conv_out = conv_out + conv_weight[offset] * shift_down(mixed, KW - 1 - offset)
        conv_flat = conv_out.reshape(rows_here, local_width)
        mixer = (gate_c * conv_flat).astype(narrow)

        inputs_mine = mine(tokens).astype(wide)
        scale_one_mine = rms_scale(inputs_mine)
        grad_mine = mine(cotangent).astype(wide)

        resid = inputs_mine + half_sum(mine(mixer), others(mixer), lambda v: product(v, out_weight))
        scale_two = rms_scale(resid)
        normed_two_mine = (resid * scale_two * norm2_gain).astype(narrow)
        normed_two = whole(normed_two_mine)

        d_act = product_back(cotangent, down_weight)
        gate_pre = product(normed_two, gate_weight)
        up_pre = product(normed_two, up_weight)
        sigma = jax.nn.sigmoid(gate_pre)
        activated = (gate_pre * sigma * up_pre).astype(narrow)
        d_gate = (d_act * up_pre * sigma * (1.0 + gate_pre * (1.0 - sigma))).astype(narrow)
        d_up = (d_act * gate_pre * sigma).astype(narrow)

        down_sum = scatter_sum(cotangent, activated, x_first, True)
        gate_sum = scatter_sum(normed_two, d_gate, x_first, False)
        up_sum = scatter_sum(normed_two, d_up, x_first, False)

        d_both = jnp.concatenate([d_gate, d_up], axis=1)
        d_normed_two = half_sum(
            mine(d_both),
            others(d_both),
            lambda v: product_back(v[:, : v.shape[1] // 2], gate_weight)
            + product_back(v[:, v.shape[1] // 2 :], up_weight),
        )
        norm2_part = jnp.sum(d_normed_two * resid * scale_two, axis=0)
        scaled_two = d_normed_two * norm2_gain
        d_resid = (
            grad_mine
            + scale_two * scaled_two
            - resid * scale_two**3 * jnp.mean(scaled_two * resid, axis=-1, keepdims=True)
        )
        d_resid_b = whole(d_resid.astype(narrow))

        out_sum = scatter_sum(d_resid_b, mixer, x_first, True)
        d_mixer = product_back(d_resid_b, out_weight)
        d_gate_c = d_mixer * conv_flat
        d_conv = (d_mixer * gate_c).reshape(sequences, SEQ, local_width)
        conv_rows = []
        d_mixed = jnp.zeros_like(mixed)
        for offset in range(KW):
            conv_rows.append(jnp.sum(d_conv * shift_down(mixed, KW - 1 - offset), axis=(0, 1)))
            d_mixed = d_mixed + conv_weight[offset] * shift_up(d_conv, KW - 1 - offset)
        conv_part = jnp.stack(conv_rows, axis=0)
        d_mixed = d_mixed.reshape(rows_here, local_width)
        d_proj = jnp.concatenate([d_mixed * values, d_gate_c, d_mixed * gate_b], axis=1).astype(narrow)
        in_sum = scatter_sum(normed_one, d_proj, x_first, False).reshape(
            model_width // n_dp, 3, local_width
        )
        d_normed_one = half_sum(mine(d_proj), others(d_proj), lambda v: product_back(v, flat_in))
        norm1_part = jnp.sum(d_normed_one * inputs_mine * scale_one_mine, axis=0)
        scaled_one = d_normed_one * norm1_gain
        d_inputs = whole(
            d_resid
            + scale_one_mine * scaled_one
            - inputs_mine
            * scale_one_mine**3
            * jnp.mean(scaled_one * inputs_mine, axis=-1, keepdims=True)
        )

        ffn = half_sum(mine(activated), others(activated), lambda v: product(v, down_weight))
        output = whole((resid + ffn).astype(narrow))

        norm_parts = all_sum(jnp.stack([norm1_part, norm2_part]), "tensor", n_tensor, [0])
        norm_parts = all_sum(norm_parts, "dp", n_dp, dp_bits)
        conv_sum = all_sum(conv_part, "dp", n_dp, dp_bits)
        return (
            output,
            d_inputs,
            norm_parts[0],
            in_sum,
            conv_sum,
            out_sum,
            norm_parts[1],
            gate_sum,
            up_sum,
            down_sum,
        )

    return body


def solution(mesh):
    placed = (
        P("dp", None),
        P(),
        P(None, None, "tensor"),
        P(None, "tensor"),
        P("tensor", None),
        P(),
        P(None, "tensor"),
        P(None, "tensor"),
        P("tensor", None),
        P("dp", None),
    )
    return jax.shard_map(
        make_body(mesh.shape["dp"], mesh.shape["tensor"]),
        mesh=mesh,
        in_specs=placed,
        out_specs=(
            P("dp", None),
            P("dp", None),
            P(),
            P("dp", None, "tensor"),
            P(None, "tensor"),
            P("tensor", "dp"),
            P(),
            P("dp", "tensor"),
            P("dp", "tensor"),
            P("tensor", "dp"),
        ),
        check_vma=False,
    )
```
